256 devices in a mesh: span: 16 (over z, x_hi), sp: 8 (over y, x_lo), fsdp: 2 (over core).
Axes of the slice: x: 4 (x_hi: 2, x_lo: 2; x = x_hi * 2 + x_lo), y: 4, z: 8, core: 2. Of those that a mesh axis runs over, the one named last changes fastest.
Arguments:
- query_pre: bfloat16 [2, 16384, 3072], P('fsdp', ('span', 'sp')), may hold values from -12 to 12
- key_pre: bfloat16 [2, 16384, 3072], P('fsdp', ('span', 'sp')), may hold values from -12 to 12
- values: bfloat16 [2, 16384, 3072], P('fsdp', ('span', 'sp')), may hold values from -6 to 6
- cotangent: bfloat16 [2, 16384, 3072], P('fsdp', ('span', 'sp')), may hold values from -6 to 6
- gains: float32 [2, 3072], P(None, 'fsdp'), may hold values from 0.5 to 1.5
- frame_span: int32 [2, 16384], P('fsdp', 'span'), may hold values from 0 to 31, as said below
- denoise_steps: int32 [2, 32], P('fsdp'), may hold values from 1 to 4
Outputs:
- query_grad: bfloat16 [2, 16384, 3072], P('fsdp', ('span', 'sp'))
- key_grad: bfloat16 [2, 16384, 3072], P('fsdp', ('span', 'sp'))
- value_grad: bfloat16 [2, 16384, 3072], P('fsdp', ('span', 'sp'))
- gain_grad: float32 [2, 3072], P(None, 'fsdp')
The draws below stay inside these ranges and needn't reach their ends.
Inputs may be any that keep to these rules, and one draw needn't show every extreme that they name: `frame_span`: never falls along a video. Group g (tokens g * 1024 to (g + 1) * 1024 - 1) holds frame spans 2 g and 2 g + 1, each from a quarter to three quarters of the group's tokens.
All inputs are finite; a program needn't handle non-finite values.
Results may differ from the reference program's by a relative error of at most 0.0081.
The reference program's roundings to bfloat16 on the way count: a program that leaves them out, or rounds other values in their place, can miss the bound.
Values may be sent and summed in bfloat16 or wider, within the bound.
No kernel may reach another device: no remote copies, remote signals or barrier semaphores. Data moves between devices by JAX's collectives and lax.ppermute only.
A program may use at most 128 MiB of HBM per device.

```python
import jax
import jax.numpy as jnp
from jax import lax

TOK_DEV = 128
HEADS = 24
HDIM = 128
CHANNELS = 3072
TOKENS = 16384
SPANS = 32
VIDEOS = 2
N_SPAN = 16
N_SP = 8


def draw_frame_span(key, part):
    block = TOK_DEV * N_SP
    bounds = jax.random.randint(key, (VIDEOS, N_SPAN), block // 4, 3 * block // 4 + 1)
    positions = jnp.arange(block, dtype=jnp.int32)
    later = (positions[None, None, :] >= bounds[:, :, None]).astype(jnp.int32)
    base = 2 * jnp.arange(N_SPAN, dtype=jnp.int32)
    return (base[None, :, None] + later).reshape(VIDEOS, TOKENS).astype(jnp.int32)


def drawn_rows(key, salt):
    third = jax.random.fold_in(jax.random.fold_in(key, salt), 2)
    return jnp.clip(jax.random.normal(third, (VIDEOS, TOKENS, CHANNELS), jnp.float32), -6.0, 6.0)


def draw_query_pre(key, part):
    rows = drawn_rows(key, 11)
    return rows.astype(jnp.bfloat16)


def draw_key_pre(key, part):
    rows = drawn_rows(key, 12)
    return rows.astype(jnp.bfloat16)


def touch_ends(values, stream_key, low, largest):
    longest = values.shape.index(max(values.shape))
    spots = []
    for shift in (0, 1):
        where = [jax.random.randint(jax.random.fold_in(stream_key, axis), (), 0, length) for axis, length in enumerate(values.shape)]
        where[longest] = (where[longest] + shift) % values.shape[longest]
        spots.append(tuple(where))
    return values.at[spots[0]].set(low).at[spots[1]].set(largest)


def block_levels(key, shape, cuts, least, top_value):
    loudness = 1.0
    for dim, blocks in cuts:
        draws = jax.random.uniform(jax.random.fold_in(jax.random.fold_in(key, 6), dim), (blocks,), jnp.float32, least / len(cuts), top_value / len(cuts))
        loudness = loudness * jnp.repeat(jnp.exp(draws), shape[dim] // blocks).reshape((-1,) + (1,) * (len(shape) - 1 - dim))
    return loudness


def centred(rng, shape, deviation, most, cuts=(), kind=jnp.bfloat16):
    array = deviation * jax.random.normal(rng, shape, jnp.float32)
    if cuts:
        array = array * block_levels(rng, shape, cuts, -0.22, 0.18)
    return jnp.clip(array, -most, most).astype(kind)


def setup_inputs(seed: int = 0) -> dict:
    key_list = jax.random.split(jax.random.key(seed), 8)
    return {
        "query_pre": draw_query_pre(jax.random.fold_in(key_list[7], 71), 0),
        "key_pre": draw_key_pre(jax.random.fold_in(key_list[7], 71), 0),
        "values": centred(key_list[2], (VIDEOS, TOKENS, CHANNELS), 1.0, 6.0, ((0, 2), (1, 128))),
        "cotangent": centred(key_list[3], (VIDEOS, TOKENS, CHANNELS), 1.0, 6.0, ((0, 2), (1, 128))),
        "gains": jnp.clip(1.0 + 0.1 * jax.random.normal(key_list[4], (2, CHANNELS), jnp.float32), 0.5, 1.5),
        "frame_span": draw_frame_span(jax.random.fold_in(key_list[7], 71), 0),
        "denoise_steps": touch_ends(jax.random.randint(key_list[6], (VIDEOS, SPANS), 1, 5), jax.random.fold_in(key_list[6], 1), 1, 4).astype(jnp.int32),
    }


EPSILON = 1e-06
NEGATIVE = -1e+30

def normed(raw_rows, gain_row):
    wide = raw_rows.astype(jnp.float32)
    inverse_rms = lax.rsqrt(lax.optimization_barrier(jnp.mean(wide * wide, axis=-1, keepdims=True)) + EPSILON)
    normal_rows = wide * inverse_rms
    return (normal_rows, inverse_rms, (normal_rows * gain_row).astype(jnp.bfloat16))

def norm_backward(grad_rows, normal_rows, inverse_rms, gain_row):
    upstream = grad_rows.astype(jnp.float32)
    scaled = upstream * gain_row
    inner = lax.optimization_barrier(jnp.mean(scaled * normal_rows, axis=-1, keepdims=True))
    result = (inverse_rms * (scaled - normal_rows * inner)).astype(jnp.bfloat16)
    return (result, lax.optimization_barrier(jnp.sum(upstream * normal_rows, axis=0)))

def across(left, right):
    return lax.dot_general(left, right, (((1,), (1,)), ((), ())), preferred_element_type=jnp.float32)

def downward(left, right):
    return lax.dot_general(left, right, (((0,), (0,)), ((), ())), preferred_element_type=jnp.float32)

def head_grads(query_head, grad_head, key_own, value_own, key_prev, value_prev, own_mask, prev_open, step_weight):
    score_scale = HDIM ** (-0.5)
    score_own = across(query_head, key_own) * score_scale
    score_prev = across(query_head, key_prev) * score_scale
    masked_own = jnp.where(own_mask, score_own, NEGATIVE)
    masked_prev = jnp.where(prev_open, score_prev, NEGATIVE)
    row_max = jnp.maximum(lax.optimization_barrier(jnp.max(masked_own, axis=1)), lax.optimization_barrier(jnp.max(masked_prev, axis=1)))
    row_total = lax.optimization_barrier(jnp.sum(jnp.exp(masked_own - row_max[:, None]), axis=1)) + lax.optimization_barrier(jnp.sum(jnp.exp(masked_prev - row_max[:, None]), axis=1))
    log_total = row_max + jnp.log(row_total)
    prob_own = jnp.where(own_mask, jnp.exp(score_own - log_total[:, None]), 0.0)
    prob_prev = jnp.where(prev_open, jnp.exp(score_prev - log_total[:, None]), 0.0)
    grad_prob_own = across(grad_head, value_own)
    grad_prob_prev = across(grad_head, value_prev)
    row_delta = lax.optimization_barrier(jnp.sum(prob_own * grad_prob_own, axis=1)) + lax.optimization_barrier(jnp.sum(prob_prev * grad_prob_prev, axis=1))
    factor = step_weight[:, None]
    sgrad_own = (factor * prob_own * (grad_prob_own - row_delta[:, None])).astype(jnp.bfloat16)
    sgrad_prev = (factor * prob_prev * (grad_prob_prev - row_delta[:, None])).astype(jnp.bfloat16)
    weight_own = (factor * prob_own).astype(jnp.bfloat16)
    weight_prev = (factor * prob_prev).astype(jnp.bfloat16)
    query_part = (jnp.dot(sgrad_own, key_own, preferred_element_type=jnp.float32) + jnp.dot(sgrad_prev, key_prev, preferred_element_type=jnp.float32)) * score_scale
    key_own_grad = downward(sgrad_own, query_head) * score_scale
    value_own_grad = downward(weight_own, grad_head)
    key_prev_grad = downward(sgrad_prev, query_head) * score_scale
    value_prev_grad = downward(weight_prev, grad_head)
    return (query_part, key_own_grad, value_own_grad, key_prev_grad, value_prev_grad)

def reference(query_pre, key_pre, values, cotangent, gains, frame_span, denoise_steps):
    block = TOK_DEV * N_SP
    gain_total = jnp.zeros((2, HEADS * HDIM), jnp.float32)
    query_outs = []
    key_outs = []
    value_outs = []

    def split_heads(rows):
        return rows.reshape(N_SPAN, block, HEADS, HDIM).transpose(0, 2, 1, 3)

    def join_heads(parts):
        return parts.transpose(0, 2, 1, 3).reshape(N_SPAN * block, HEADS * HDIM)
    for video in range(VIDEOS):
        q_normal, q_inverse, q_ready = normed(query_pre[video], gains[0])
        k_normal, k_inverse, k_ready = normed(key_pre[video], gains[1])
        span_ids = frame_span[video]
        step_weight = denoise_steps[video][span_ids].astype(jnp.float32)
        query_heads = split_heads(q_ready)
        key_heads = split_heads(k_ready)
        value_heads = split_heads(values[video])
        grad_heads = split_heads(cotangent[video])
        results = []
        for group_index in range(N_SPAN):
            earlier = max(group_index - 1, 0)
            ids_here = span_ids[group_index * block:(group_index + 1) * block]
            own_mask = ids_here[None, :] <= ids_here[:, None]
            weight_here = step_weight[group_index * block:(group_index + 1) * block]
            prev_open = group_index > 0

            def one_head(operands, own_mask=own_mask, prev_open=prev_open, weight_here=weight_here):
                query_head, grad_head, key_own, value_own, key_prev, value_prev = operands
                return head_grads(query_head, grad_head, key_own, value_own, key_prev, value_prev, own_mask, prev_open, weight_here)
            results.append(lax.map(one_head, (query_heads[group_index], grad_heads[group_index], key_heads[group_index], value_heads[group_index], key_heads[earlier], value_heads[earlier])))
        query_parts = []
        key_parts = []
        value_parts = []
        for group_index in range(N_SPAN):
            key_sum = results[group_index][1]
            value_sum = results[group_index][2]
            if group_index + 1 < N_SPAN:
                key_sum = key_sum + results[group_index + 1][3]
                value_sum = value_sum + results[group_index + 1][4]
            query_parts.append(results[group_index][0].astype(jnp.bfloat16))
            key_parts.append(key_sum.astype(jnp.bfloat16))
            value_parts.append(value_sum.astype(jnp.bfloat16))
        query_attn = join_heads(jnp.stack(query_parts))
        key_attn = join_heads(jnp.stack(key_parts))
        value_attn = join_heads(jnp.stack(value_parts))
        query_back, query_gain = norm_backward(query_attn, q_normal, q_inverse, gains[0])
        key_back, key_gain = norm_backward(key_attn, k_normal, k_inverse, gains[1])
        gain_total = gain_total + jnp.stack([query_gain, key_gain])
        query_outs.append(query_back)
        key_outs.append(key_back)
        value_outs.append(value_attn)
    return (jnp.stack(query_outs), jnp.stack(key_outs), jnp.stack(value_outs), gain_total)
```

```python
import functools

import jax
import jax.numpy as jnp
import numpy as np
from jax import lax
from jax.experimental import pallas as pl
from jax.experimental.pallas import tpu as pltpu
from jax.sharding import PartitionSpec as P

HDIM = 128
TOK = 128
GROUP = 1024
QTILE = 256
KCHUNK = 256
EPSILON = 1e-06
NEGATIVE = -1e30
LOG2E = 1.4426950408889634
SCALE = HDIM ** (-0.5)
F32 = jnp.float32
BF16 = jnp.bfloat16


def nt(left, right):
    return lax.dot_general(left, right, (((1,), (1,)), ((), ())), preferred_element_type=F32)


def nn(left, right):
    return lax.dot_general(left, right, (((1,), (0,)), ((), ())), preferred_element_type=F32)


def pack_kernel(heads_a, q_ref, k_ref, v_ref, g_ref, gain_ref, a_ref, b_ref):
    heads = q_ref.shape[1] // HDIM

    def put(slot, rows):
        for head in range(heads):
            piece = rows[:, head * HDIM : (head + 1) * HDIM]
            if head < heads_a:
                a_ref[head, slot] = piece
            else:
                b_ref[head - heads_a, slot] = piece

    for slot, ref in ((0, q_ref), (1, k_ref)):
        wide = ref[...].astype(F32)
        inverse = lax.rsqrt(jnp.mean(wide * wide, axis=1, keepdims=True) + EPSILON)
        put(slot, (wide * inverse * gain_ref[slot : slot + 1, :]).astype(BF16))
    put(2, v_ref[...])
    put(3, g_ref[...])


def pack(query_pre, key_pre, values, cotangent, gain_full, heads_a):
    tokens, channels = query_pre.shape
    heads_b = channels // HDIM - heads_a
    step = 32
    rows = pl.BlockSpec((step, channels), lambda i: (i, 0))
    return pl.pallas_call(
        functools.partial(pack_kernel, heads_a),
        grid=(tokens // step,),
        in_specs=[rows] * 4 + [pl.BlockSpec((2, channels), lambda i: (0, 0))],
        out_specs=[
            pl.BlockSpec((heads_a, 4, step, HDIM), lambda i: (0, 0, i, 0)),
            pl.BlockSpec((heads_b, 4, step, HDIM), lambda i: (0, 0, i, 0)),
        ],
        out_shape=[
            jax.ShapeDtypeStruct((heads_a, 4, tokens, HDIM), BF16),
            jax.ShapeDtypeStruct((heads_b, 4, tokens, HDIM), BF16),
        ],
        name="pack",
        cost_estimate=pl.CostEstimate(
            flops=10 * tokens * channels, bytes_accessed=16 * tokens * channels, transcendentals=tokens
        ),
    )(query_pre, key_pre, values, cotangent, gain_full)


def unit_kernel(
    info_ref, q_ref, g_ref, ko_ref, vo_ref, kp_ref, vp_ref,
    dq_ref, dko_ref, dvo_ref, dkp_ref, dvp_ref,
    k_ref, v_ref, kt_ref, s_ref, dp_ref, dk_ref, dv_ref,
):
    step = pl.program_id(0)
    chunks = 2 * GROUP // KCHUNK
    own_chunks = GROUP // KCHUNK

    @pl.when(step == 0)
    def _():
        k_ref[:GROUP] = ko_ref[...].reshape(GROUP, HDIM)
        k_ref[GROUP:] = kp_ref[...].reshape(GROUP, HDIM)
        v_ref[:GROUP] = vo_ref[...].reshape(GROUP, HDIM)
        v_ref[GROUP:] = vp_ref[...].reshape(GROUP, HDIM)
        kt_ref[...] = k_ref[...].T
        dk_ref[...] = jnp.zeros_like(dk_ref)
        dv_ref[...] = jnp.zeros_like(dv_ref)

    bound = info_ref[0]
    is_open = info_ref[1] > 0
    early_weight = info_ref[2].astype(F32)
    late_weight = info_ref[3].astype(F32)
    q = q_ref[...].reshape(QTILE, HDIM)
    g = g_ref[...].reshape(QTILE, HDIM)
    place = step * QTILE + lax.broadcasted_iota(jnp.int32, (1, QTILE), 1)
    early = place < bound
    reach = jnp.where(early, bound, GROUP)
    weight = jnp.where(early, early_weight, late_weight)
    factor = SCALE * LOG2E

    own_max = None
    prev_max = None
    for chunk in range(chunks):
        span = slice(chunk * KCHUNK, (chunk + 1) * KCHUNK)
        scores = nt(k_ref[span], q)
        if 0 < chunk < own_chunks:
            row = chunk * KCHUNK + lax.broadcasted_iota(jnp.int32, (KCHUNK, QTILE), 0)
            scores = jnp.where(row < reach, scores, NEGATIVE)
        s_ref[span] = scores
        top = jnp.max(scores, axis=0, keepdims=True)
        if chunk < own_chunks:
            own_max = top if own_max is None else jnp.maximum(own_max, top)
        else:
            prev_max = top if prev_max is None else jnp.maximum(prev_max, top)
    row_max = jnp.maximum(own_max, jnp.where(is_open, prev_max, NEGATIVE)) * factor
    prev_shift = jnp.where(is_open, row_max, -NEGATIVE)
    total = jnp.zeros((1, QTILE), F32)
    inner = jnp.zeros((1, QTILE), F32)
    for chunk in range(chunks):
        span = slice(chunk * KCHUNK, (chunk + 1) * KCHUNK)
        shift = row_max if chunk < own_chunks else prev_shift
        probs = jnp.exp2(s_ref[span] * factor - shift)
        total = total + jnp.sum(probs, axis=0, keepdims=True)
        grads = nt(v_ref[span], g)
        inner = inner + jnp.sum(probs * grads, axis=0, keepdims=True)
        s_ref[span] = probs
        dp_ref[span] = grads
    over = 1.0 / total
    delta = inner * over
    scaled = weight * over
    dq_t = jnp.zeros((HDIM, QTILE), F32)
    for chunk in range(chunks):
        span = slice(chunk * KCHUNK, (chunk + 1) * KCHUNK)
        weights = s_ref[span] * scaled
        sgrad = (weights * (dp_ref[span] - delta)).astype(BF16)
        dk_ref[span] += nn(sgrad, q)
        dv_ref[span] += nn(weights.astype(BF16), g)
        dq_t = dq_t + nn(kt_ref[:, span], sgrad)
    dq_ref[...] = (dq_t * SCALE).T.astype(BF16).reshape(dq_ref.shape)

    @pl.when(step == pl.num_programs(0) - 1)
    def _():
        dko_ref[...] = dk_ref[:GROUP] * SCALE
        dvo_ref[...] = dv_ref[:GROUP]
        dkp_ref[...] = (dk_ref[GROUP:] * SCALE).astype(BF16)
        dvp_ref[...] = dv_ref[GROUP:].astype(BF16)


def unit(info, own, own_at, prev, prev_at, prev_slots, name):
    slabs = GROUP // TOK
    tiles = QTILE // TOK

    def whole(at, slot):
        return pl.BlockSpec((slabs, 1, TOK, HDIM), lambda i: (at, slot, 0, 0))

    def tiled(slot):
        first = own_at * slabs // tiles
        return pl.BlockSpec((tiles, 1, TOK, HDIM), lambda i: (first + i, slot, 0, 0))

    full = pl.BlockSpec((GROUP, HDIM), lambda i: (0, 0))
    return pl.pallas_call(
        unit_kernel,
        grid=(GROUP // QTILE,),
        in_specs=[
            pl.BlockSpec(memory_space=pltpu.SMEM),
            tiled(0), tiled(3), whole(own_at, 1), whole(own_at, 2),
            whole(prev_at, prev_slots[0]), whole(prev_at, prev_slots[1]),
        ],
        out_specs=[pl.BlockSpec((QTILE, HDIM), lambda i: (i, 0)), full, full, full, full],
        out_shape=[
            jax.ShapeDtypeStruct((GROUP, HDIM), BF16),
            jax.ShapeDtypeStruct((GROUP, HDIM), F32),
            jax.ShapeDtypeStruct((GROUP, HDIM), F32),
            jax.ShapeDtypeStruct((GROUP, HDIM), BF16),
            jax.ShapeDtypeStruct((GROUP, HDIM), BF16),
        ],
        scratch_shapes=[
            pltpu.VMEM((2 * GROUP, HDIM), BF16),
            pltpu.VMEM((2 * GROUP, HDIM), BF16),
            pltpu.VMEM((HDIM, 2 * GROUP), BF16),
            pltpu.VMEM((2 * GROUP, QTILE), F32),
            pltpu.VMEM((2 * GROUP, QTILE), F32),
            pltpu.VMEM((2 * GROUP, HDIM), F32),
            pltpu.VMEM((2 * GROUP, HDIM), F32),
        ],
        name=name,
        cost_estimate=pl.CostEstimate(
            flops=20 * GROUP * GROUP * HDIM, bytes_accessed=3 << 20, transcendentals=2 * GROUP * GROUP
        ),
    )(info, own, own, own, own, prev, prev)


def combine_kernel(groups, own_ref, *refs):
    ins, (out_ref, gain_ref) = refs[: 5 * groups], refs[5 * groups :]
    slabs = GROUP // TOK
    gain_q = jnp.zeros((1, HDIM), F32)
    gain_k = jnp.zeros((1, HDIM), F32)
    for group in range(groups):
        dq, dk, dv, dk_more, dv_more = ins[5 * group : 5 * group + 5]
        at = slice(group * slabs, (group + 1) * slabs)
        q = own_ref[at, 0].reshape(GROUP, HDIM).astype(F32)
        k = own_ref[at, 1].reshape(GROUP, HDIM).astype(F32)
        dq_all = dq[...]
        dk_all = (dk[...] + dk_more[...].astype(F32)).astype(BF16)
        dv_all = (dv[...] + dv_more[...].astype(F32)).astype(BF16)
        gain_q = gain_q + jnp.sum(dq_all.astype(F32) * q, axis=0, keepdims=True)
        gain_k = gain_k + jnp.sum(dk_all.astype(F32) * k, axis=0, keepdims=True)
        out_ref[at, 0] = dq_all.reshape(slabs, TOK, HDIM)
        out_ref[at, 1] = dk_all.reshape(slabs, TOK, HDIM)
        out_ref[at, 2] = dv_all.reshape(slabs, TOK, HDIM)
    gain_ref[0:1] = gain_q
    gain_ref[1:2] = gain_k


def combine(own, parts, name):
    groups = len(parts)
    slabs = groups * GROUP // TOK
    flat = [array for part in parts for array in part]
    full = pl.BlockSpec((GROUP, HDIM), lambda i: (0, 0))
    return pl.pallas_call(
        functools.partial(combine_kernel, groups),
        grid=(1,),
        in_specs=[pl.BlockSpec((slabs, 2, TOK, HDIM), lambda i: (0, 0, 0, 0))] + [full] * len(flat),
        out_specs=[
            pl.BlockSpec((slabs, 3, TOK, HDIM), lambda i: (0, 0, 0, 0)),
            pl.BlockSpec((2, HDIM), lambda i: (0, 0)),
        ],
        out_shape=[
            jax.ShapeDtypeStruct((slabs, 3, TOK, HDIM), BF16),
            jax.ShapeDtypeStruct((2, HDIM), F32),
        ],
        name=name,
        cost_estimate=pl.CostEstimate(
            flops=10 * groups * GROUP * HDIM, bytes_accessed=groups * GROUP * HDIM * 20, transcendentals=0
        ),
    )(own, *flat)


def finish_kernel(heads_a, heads_b, x_ref, y_ref, gain_ref, a_ref, b_ref, qg_ref, kg_ref, vg_ref):
    channels = x_ref.shape[1]

    def piece(head, slot):
        return a_ref[head, slot] if head < heads_a else b_ref[head - heads_a, slot]

    for slot, ref, out in ((0, x_ref, qg_ref), (1, y_ref, kg_ref)):
        wide = ref[...].astype(F32)
        inverse = lax.rsqrt(jnp.mean(wide * wide, axis=1, keepdims=True) + EPSILON)
        normal = wide * inverse
        up = jnp.concatenate([piece(h, slot).astype(F32) for h in range(heads_a + heads_b)], axis=1)
        scaled = up * gain_ref[slot : slot + 1, :]
        inner = jnp.sum(scaled * normal, axis=1, keepdims=True) * (1.0 / channels)
        out[...] = (inverse * (scaled - normal * inner)).astype(BF16)
    for head in range(heads_a + heads_b):
        vg_ref[:, head * HDIM : (head + 1) * HDIM] = piece(head, 2)


def finish(query_pre, key_pre, gain_full, back_a, back_b):
    tokens, channels = query_pre.shape
    heads_a, heads_b = back_a.shape[0], back_b.shape[0]
    step = 32
    rows = pl.BlockSpec((step, channels), lambda i: (i, 0))
    return pl.pallas_call(
        functools.partial(finish_kernel, heads_a, heads_b),
        grid=(tokens // step,),
        in_specs=[
            rows, rows,
            pl.BlockSpec((2, channels), lambda i: (0, 0)),
            pl.BlockSpec((heads_a, 3, step, HDIM), lambda i: (0, 0, i, 0)),
            pl.BlockSpec((heads_b, 3, step, HDIM), lambda i: (0, 0, i, 0)),
        ],
        out_specs=[rows] * 3,
        out_shape=[jax.ShapeDtypeStruct((tokens, channels), BF16)] * 3,
        name="finish",
        cost_estimate=pl.CostEstimate(
            flops=30 * tokens * channels, bytes_accessed=16 * tokens * channels, transcendentals=tokens
        ),
    )(query_pre, key_pre, gain_full, back_a, back_b)


def shifted(value, steps, count):
    first, last = (max(0, -steps), min(count, count - steps))
    return lax.ppermute(value, "span", [(source, source + steps) for source in range(first, last)])


def on_device(query_pre, key_pre, values, cotangent, gains, frame_span, denoise_steps):
    n_span, n_sp = lax.axis_size("span"), lax.axis_size("sp")
    heads_a = 2 * n_sp
    slabs = GROUP // TOK
    plane = [[first + i for i in range(heads_a)] for first in range(0, n_span * n_sp, heads_a)]
    to_plane = functools.partial(
        lax.all_to_all, axis_name=("span", "sp"), split_axis=0, concat_axis=0, tiled=True, axis_index_groups=plane
    )
    to_sp = functools.partial(lax.all_to_all, axis_name="sp", split_axis=0, concat_axis=0, tiled=True)

    span = lax.axis_index("span")
    gain_full = lax.all_gather(gains, "fsdp", axis=1, tiled=True)
    send_a, send_b = pack(query_pre[0], key_pre[0], values[0], cotangent[0], gain_full, heads_a)
    own_b = to_sp(send_b)
    own_a = to_plane(send_a)

    ids = frame_span[0]
    bound = jnp.sum((ids == ids[0]).astype(jnp.int32))
    other = lax.ppermute(
        jnp.full((8, 128), bound, F32), "span", [(i, i ^ 1) for i in range(n_span)]
    )[0, 0].astype(jnp.int32)
    odd = span % 2
    table = denoise_steps[0]
    even_bound = jnp.where(odd == 0, bound, other)
    odd_bound = jnp.where(odd == 0, other, bound)

    def info_of(limit, group):
        weights = lax.dynamic_slice(table, (2 * group,), (2,))
        return jnp.stack([limit, (group > 0).astype(jnp.int32), weights[0], weights[1]])

    even = span - odd

    prev_b = shifted(own_b[:, 1:3], 1, n_span)
    dq_b, dk_b, dv_b, dk_b_prev, dv_b_prev = unit(info_of(bound, span), own_b, 0, prev_b, 0, (0, 1), "unit_b")
    back_b = shifted(jnp.concatenate([dk_b_prev, dv_b_prev], axis=0), -1, n_span)
    out_b, gain_b = combine(own_b, [(dq_b, dk_b, dv_b, back_b[:GROUP], back_b[GROUP:])], "combine_b")
    home_b = to_sp(out_b)

    prev_a = shifted(own_a[slabs:, 1:3], 2, n_span)
    dq_o, dk_o, dv_o, dk_o_prev, dv_o_prev = unit(info_of(odd_bound, even + 1), own_a, 1, own_a, 0, (1, 2), "unit_o")
    dq_e, dk_e, dv_e, dk_e_prev, dv_e_prev = unit(info_of(even_bound, even), own_a, 0, prev_a, 0, (0, 1), "unit_e")
    back_a = shifted(jnp.concatenate([dk_e_prev, dv_e_prev], axis=0), -2, n_span)
    out_a, gain_a = combine(
        own_a,
        [(dq_e, dk_e, dv_e, dk_o_prev, dv_o_prev), (dq_o, dk_o, dv_o, back_a[:GROUP], back_a[GROUP:])],
        "combine_a",
    )
    home_a = to_plane(out_a)

    share = jnp.concatenate([gain_a, gain_b, jnp.zeros((4, HDIM), F32)], axis=0)
    share = share + lax.ppermute(share, "fsdp", [(0, 1), (1, 0)])
    reach = 2
    while reach < n_span:
        share = share + lax.ppermute(share, "span", [(i, i ^ reach) for i in range(n_span)])
        reach *= 2
    across = lax.ppermute(share, "span", [(i, i ^ 1) for i in range(n_span)])
    share = jnp.concatenate([share[:2], share[2:] + across[2:]], axis=0)
    shares = to_plane(jnp.broadcast_to(share[None], (heads_a, 8, HDIM)))
    total = jnp.stack(
        [
            jnp.concatenate([shares[:, row].reshape(-1), shares[:n_sp, 2 + row].reshape(-1)])
            for row in range(2)
        ]
    )
    half = gains.shape[1]
    mine = jnp.where(lax.axis_index("fsdp") == 0, total[:, :half], total[:, half:])
    gain_grad = mine / gains

    query_back, key_back, value_back = finish(query_pre[0], key_pre[0], gain_full, home_a, home_b)
    return (query_back[None], key_back[None], value_back[None], gain_grad)


def solution(mesh):
    rows = P("fsdp", ("span", "sp"), None)
    return jax.shard_map(
        on_device,
        mesh=mesh,
        in_specs=(rows, rows, rows, rows, P(None, "fsdp"), P("fsdp", "span"), P("fsdp", None)),
        out_specs=(rows, rows, rows, P(None, "fsdp")),
        check_vma=False,
    )
```

```python
import functools

import jax
import jax.numpy as jnp
from jax import lax
from jax.experimental import pallas as pl
from jax.experimental.pallas import tpu as pltpu
from jax.sharding import PartitionSpec as P


HDIM = 128
TOK = 128
GROUP = 1024
KCHUNK = 512
EPSILON = 1e-06
NEGATIVE = -1e30
LOG2E = 1.4426950408889634
SCALE = HDIM ** (-0.5)
F32 = jnp.float32
BF16 = jnp.bfloat16


def nt(left, right):
    return lax.dot_general(left, right, (((1,), (1,)), ((), ())), preferred_element_type=F32)


def nn(left, right):
    return lax.dot_general(left, right, (((1,), (0,)), ((), ())), preferred_element_type=F32)


def pack_kernel(heads_a, q_ref, k_ref, v_ref, g_ref, gain_ref, kv_ref, qg_ref, b_ref):
    heads = q_ref.shape[1] // HDIM

    def put(ref, slot_a, slot_b, rows):
        for head in range(heads):
            piece = rows[:, head * HDIM : (head + 1) * HDIM]
            if head < heads_a:
                ref[head, slot_a] = piece
            else:
                b_ref[head - heads_a, slot_b] = piece

    def normed(ref, row):
        wide = ref[...].astype(F32)
        inverse = lax.rsqrt(jnp.mean(wide * wide, axis=1, keepdims=True) + EPSILON)
        return (wide * inverse * gain_ref[row : row + 1, :]).astype(BF16)

    put(kv_ref, 0, 0, normed(k_ref, 1))
    put(kv_ref, 1, 1, v_ref[...])
    put(qg_ref, 0, 2, normed(q_ref, 0))
    put(qg_ref, 1, 3, g_ref[...])


def pack(query_pre, key_pre, values, cotangent, gain_full, heads_a):
    tokens, channels = query_pre.shape
    heads_b = channels // HDIM - heads_a
    step = 32
    rows = pl.BlockSpec((step, channels), lambda i: (i, 0))

    def slabs(heads, slots):
        return pl.BlockSpec((heads, slots, step, HDIM), lambda i: (0, 0, i, 0))

    return pl.pallas_call(
        functools.partial(pack_kernel, heads_a),
        grid=(tokens // step,),
        in_specs=[rows] * 4 + [pl.BlockSpec((2, channels), lambda i: (0, 0))],
        out_specs=[slabs(heads_a, 2), slabs(heads_a, 2), slabs(heads_b, 4)],
        out_shape=[
            jax.ShapeDtypeStruct((heads_a, 2, tokens, HDIM), BF16),
            jax.ShapeDtypeStruct((heads_a, 2, tokens, HDIM), BF16),
            jax.ShapeDtypeStruct((heads_b, 4, tokens, HDIM), BF16),
        ],
        name="pack",
        cost_estimate=pl.CostEstimate(
            flops=10 * tokens * channels, bytes_accessed=16 * tokens * channels, transcendentals=tokens
        ),
    )(query_pre, key_pre, values, cotangent, gain_full)


def unit_kernel(
    line, info_ref, q_ref, g_ref, ko_ref, vo_ref, kp_ref, vp_ref,
    dq_ref, dko_ref, dvo_ref, back_ref, gain_ref,
    p_ref, dp_ref,
):
    chunks = 2 * GROUP // KCHUNK
    own_chunks = GROUP // KCHUNK

    def part_of(own_ref, prev_ref, chunk):
        ref = own_ref if chunk < own_chunks else prev_ref
        first = chunk % own_chunks * KCHUNK // TOK
        return ref[first : first + KCHUNK // TOK].reshape(KCHUNK, HDIM)

    keys_at = functools.partial(part_of, ko_ref, kp_ref)
    values_at = functools.partial(part_of, vo_ref, vp_ref)
    bound = info_ref[line, 0]
    is_open = info_ref[line, 1] > 0
    early_weight = info_ref[line, 2].astype(F32)
    late_weight = info_ref[line, 3].astype(F32)
    q = q_ref[...].reshape(GROUP, HDIM)
    g = g_ref[...].reshape(GROUP, HDIM)
    early = lax.broadcasted_iota(jnp.int32, (1, GROUP), 1) < bound
    reach = jnp.where(early, bound, GROUP)
    weight = jnp.where(early, early_weight, late_weight)
    factor = SCALE * LOG2E

    pieces = []
    for chunk in range(chunks):
        span = slice(chunk * KCHUNK, (chunk + 1) * KCHUNK)
        scores = nt(keys_at(chunk), q)
        if chunk < own_chunks and (chunk + 1) * KCHUNK > GROUP // 4:
            row = chunk * KCHUNK + lax.broadcasted_iota(jnp.int32, (KCHUNK, GROUP), 0)
            scores = jnp.where(row < reach, scores, NEGATIVE)
        top = jnp.max(scores, axis=0, keepdims=True) * factor
        probs = jnp.exp2(scores * factor - top)
        grads = nt(values_at(chunk), g)
        p_ref[span] = probs
        dp_ref[span] = grads
        if chunk >= own_chunks:
            top = jnp.where(is_open, top, NEGATIVE)
        pieces.append((top, jnp.sum(probs, axis=0, keepdims=True), jnp.sum(probs * grads, axis=0, keepdims=True)))
    row_max = functools.reduce(jnp.maximum, [piece[0] for piece in pieces])
    lifts = [jnp.exp2(piece[0] - row_max) for piece in pieces]
    total = sum(lift * piece[1] for lift, piece in zip(lifts, pieces))
    inner = sum(lift * piece[2] for lift, piece in zip(lifts, pieces))
    over = 1.0 / total
    delta = inner * over
    dq_t = jnp.zeros((HDIM, GROUP), F32)
    for chunk in range(chunks):
        span = slice(chunk * KCHUNK, (chunk + 1) * KCHUNK)
        weights = p_ref[span] * (weight * over * lifts[chunk])
        sgrad = (weights * (dp_ref[span] - delta)).astype(BF16)
        dk = nn(sgrad, q) * SCALE
        dv = nn(weights.astype(BF16), g)
        if chunk < own_chunks:
            dko_ref[span] = dk
            dvo_ref[span] = dv
        else:
            back_ref[chunk * KCHUNK - GROUP : (chunk + 1) * KCHUNK - GROUP] = dk.astype(BF16)
            back_ref[chunk * KCHUNK : (chunk + 1) * KCHUNK] = dv.astype(BF16)
        dq_t = dq_t + nn(keys_at(chunk).T, sgrad)
    dq = (dq_t * SCALE).T
    gain_ref[...] = jnp.broadcast_to(jnp.sum(dq * q.astype(F32), axis=0, keepdims=True), (8, HDIM))
    dq_ref[...] = dq.astype(BF16)


def unit(line, info, queries, own, prev):
    slabs = GROUP // TOK

    def whole(source, which):
        _, at, slots = source
        return pl.BlockSpec((slabs, None, TOK, HDIM), lambda i: (at, slots[which], 0, 0))

    full = pl.BlockSpec((GROUP, HDIM), lambda i: (0, 0))
    return pl.pallas_call(
        functools.partial(unit_kernel, line),
        grid=(1,),
        in_specs=[pl.BlockSpec(memory_space=pltpu.SMEM)]
        + [whole(source, which) for source in (queries, own, prev) for which in (0, 1)],
        out_specs=[
            full, full, full,
            pl.BlockSpec((2 * GROUP, HDIM), lambda i: (0, 0)),
            pl.BlockSpec((8, HDIM), lambda i: (0, 0)),
        ],
        out_shape=[
            jax.ShapeDtypeStruct((GROUP, HDIM), BF16),
            jax.ShapeDtypeStruct((GROUP, HDIM), F32),
            jax.ShapeDtypeStruct((GROUP, HDIM), F32),
            jax.ShapeDtypeStruct((2 * GROUP, HDIM), BF16),
            jax.ShapeDtypeStruct((8, HDIM), F32),
        ],
        scratch_shapes=[
            pltpu.VMEM((2 * GROUP, GROUP), F32),
            pltpu.VMEM((2 * GROUP, GROUP), F32),
        ],
        cost_estimate=pl.CostEstimate(
            flops=20 * GROUP * GROUP * HDIM, bytes_accessed=3 << 20, transcendentals=2 * GROUP * GROUP
        ),
    )(info, queries[0], queries[0], own[0], own[0], prev[0], prev[0])


def combine_kernel(groups, *refs):
    ins, out_ref = refs[: 4 * groups], refs[-1]
    slabs = out_ref.shape[0] // groups
    for group in range(groups):
        dq, dk, dv, back = ins[4 * group : 4 * group + 4]
        at = slice(group * slabs, (group + 1) * slabs)
        out_ref[at, :TOK] = dq[...].reshape(slabs, TOK, HDIM)
        out_ref[at, TOK : 2 * TOK] = (dk[...] + back[:GROUP].astype(F32)).astype(BF16).reshape(slabs, TOK, HDIM)
        out_ref[at, 2 * TOK : 3 * TOK] = (dv[...] + back[GROUP:].astype(F32)).astype(BF16).reshape(slabs, TOK, HDIM)


def combine(parts):
    groups = len(parts)
    slabs = groups * GROUP // TOK
    flat = [array for part in parts for array in part]
    full = pl.BlockSpec((GROUP, HDIM), lambda i: (0, 0))
    back = pl.BlockSpec((2 * GROUP, HDIM), lambda i: (0, 0))
    specs = [full, full, full, back] * groups
    depth = 3 * TOK
    return pl.pallas_call(
        functools.partial(combine_kernel, groups),
        grid=(1,),
        in_specs=specs,
        out_specs=pl.BlockSpec((slabs, depth, HDIM), lambda i: (0, 0, 0)),
        out_shape=jax.ShapeDtypeStruct((slabs, depth, HDIM), BF16),
        cost_estimate=pl.CostEstimate(
            flops=10 * groups * GROUP * HDIM, bytes_accessed=groups * GROUP * HDIM * 20, transcendentals=0
        ),
    )(*flat)


def finish_kernel(heads_a, heads_b, x_ref, y_ref, gain_ref, *refs):
    blocks, (qg_ref, kg_ref, vg_ref) = refs[:6], refs[6:]
    channels = x_ref.shape[1]

    def piece(head, slot):
        return blocks[slot][head] if head < heads_a else blocks[3 + slot][head - heads_a]

    for slot, ref, out in ((0, x_ref, qg_ref), (1, y_ref, kg_ref)):
        wide = ref[...].astype(F32)
        inverse = lax.rsqrt(jnp.mean(wide * wide, axis=1, keepdims=True) + EPSILON)
        normal = wide * inverse
        up = jnp.concatenate([piece(h, slot).astype(F32) for h in range(heads_a + heads_b)], axis=1)
        scaled = up * gain_ref[slot : slot + 1, :]
        inner = jnp.sum(scaled * normal, axis=1, keepdims=True) * (1.0 / channels)
        out[...] = (inverse * (scaled - normal * inner)).astype(BF16)
    for head in range(heads_a + heads_b):
        vg_ref[:, head * HDIM : (head + 1) * HDIM] = piece(head, 2)


def finish(query_pre, key_pre, gain_full, home_a, home_b):
    tokens, channels = query_pre.shape
    heads_a, heads_b = home_a.shape[0], home_b.shape[0]
    step = 32
    rows = pl.BlockSpec((step, channels), lambda i: (i, 0))

    def block(heads, slot):
        return pl.BlockSpec((heads, step, HDIM), lambda i: (0, slot * (tokens // step) + i, 0))

    return pl.pallas_call(
        functools.partial(finish_kernel, heads_a, heads_b),
        grid=(tokens // step,),
        in_specs=[rows, rows, pl.BlockSpec((2, channels), lambda i: (0, 0))]
        + [block(heads_a, slot) for slot in range(3)]
        + [block(heads_b, slot) for slot in range(3)],
        out_specs=[rows] * 3,
        out_shape=[jax.ShapeDtypeStruct((tokens, channels), BF16)] * 3,
        name="finish",
        cost_estimate=pl.CostEstimate(
            flops=30 * tokens * channels, bytes_accessed=16 * tokens * channels, transcendentals=tokens
        ),
    )(query_pre, key_pre, gain_full, home_a, home_a, home_a, home_b, home_b, home_b)


def shifted(value, steps, count):
    first, last = (max(0, -steps), min(count, count - steps))
    return lax.ppermute(value, "span", [(source, source + steps) for source in range(first, last)])


def swapped(value, axis, bit, count):
    return lax.ppermute(value, axis, [(i, i ^ bit) for i in range(count)])


def lines_of(bound, other, span, table):
    odd = span % 2
    even = span - odd
    row = lax.iota(jnp.int32, 3)
    groups = jnp.where(row == 0, span, even + row - 1)
    bounds = jnp.where((row == 0) | (groups == span), bound, other)
    spans = 2 * groups[:, None] + lax.iota(jnp.int32, 8)[None, :] - 2
    match = spans[:, :, None] == lax.iota(jnp.int32, table.shape[0])[None, None, :]
    weights = jnp.sum(jnp.where(match, table[None, None, :], 0), axis=2)
    column = lax.iota(jnp.int32, 8)[None, :]
    opens = (groups > 0).astype(jnp.int32)
    return jnp.where(column == 0, bounds[:, None], jnp.where(column == 1, opens[:, None], weights))


def on_device(query_pre, key_pre, values, cotangent, gains, frame_span, denoise_steps):
    n_span, n_sp = lax.axis_size("span"), lax.axis_size("sp")
    heads_a = 2 * n_sp
    slabs = GROUP // TOK
    plane = [[first + i for i in range(heads_a)] for first in range(0, n_span * n_sp, heads_a)]

    def to_plane(value):
        return lax.all_to_all(
            value, ("span", "sp"), split_axis=0, concat_axis=0, tiled=True, axis_index_groups=plane
        )

    def to_sp(value):
        return lax.all_to_all(value, "sp", split_axis=0, concat_axis=0, tiled=True)

    span = lax.axis_index("span")
    gain_full = lax.all_gather(gains, "fsdp", axis=1, tiled=True)
    send_kv, send_qg, send_b = pack(query_pre[0], key_pre[0], values[0], cotangent[0], gain_full, heads_a)
    own_b = to_sp(send_b)
    kv = to_plane(send_kv)
    qg = to_plane(send_qg)

    ids = frame_span[0]
    bound = jnp.sum((ids == ids[0]).astype(jnp.int32))
    other = swapped(jnp.full((8, HDIM), bound, F32), "span", 1, n_span)[0, 0].astype(jnp.int32)
    info = lines_of(bound, other, span, denoise_steps[0])

    prev_b = shifted(own_b[:, 0:2], 1, n_span)
    dq_b, dk_b, dv_b, term_b, gain_b = unit(0, info, (own_b, 0, (2, 3)), (own_b, 0, (0, 1)), (prev_b, 0, (0, 1)))
    back_b = shifted(term_b, -1, n_span)
    out_b = combine([(dq_b, dk_b, dv_b, back_b)])
    home_b = to_sp(out_b)

    prev_a = shifted(kv[slabs:], 2, n_span)
    dq_e, dk_e, dv_e, term_e, gain_e = unit(1, info, (qg, 0, (0, 1)), (kv, 0, (0, 1)), (prev_a, 0, (0, 1)))
    back_a = shifted(term_e, -2, n_span)
    dq_o, dk_o, dv_o, term_o, gain_o = unit(2, info, (qg, 1, (0, 1)), (kv, 1, (0, 1)), (kv, 0, (0, 1)))

    out_a = combine([(dq_e, dk_e, dv_e, term_o), (dq_o, dk_o, dv_o, back_a)])
    home_a = to_plane(out_a)

    share = jnp.concatenate([gain_e[0:1] + gain_o[0:1], gain_b[0:1], jnp.zeros((6, HDIM), F32)], axis=0)
    share = share + swapped(share, "fsdp", 1, 2)
    reach = 2
    while reach < n_span:
        share = share + swapped(share, "span", reach, n_span)
        reach *= 2
    lines = to_plane(jnp.broadcast_to(share[None], (heads_a, 8, HDIM)))
    table = jnp.concatenate([lines[:, 0], lines[:n_sp, 1] + lines[n_sp:, 1]], axis=0)
    half = heads_a + n_sp >> 1
    mine = jnp.where(lax.axis_index("fsdp") == 0, table[:half], table[half:]).reshape(1, half * HDIM)
    gain_grad = mine / gains

    query_back, key_back, value_back = finish(query_pre[0], key_pre[0], gain_full, home_a, home_b)
    return (query_back[None], key_back[None], value_back[None], gain_grad)


def solution(mesh):
    rows = P("fsdp", ("span", "sp"), None)
    return jax.shard_map(
        on_device,
        mesh=mesh,
        in_specs=(rows, rows, rows, rows, P(None, "fsdp"), P("fsdp", "span"), P("fsdp", None)),
        out_specs=(rows, rows, rows, P(None, "fsdp")),
        check_vma=False,
    )
```

```python
import functools

import jax
import jax.numpy as jnp
from jax import lax
from jax.experimental import pallas as pl
from jax.experimental.pallas import tpu as pltpu
from jax.sharding import PartitionSpec as P


HDIM = 128
GAIN_ROWS = 3
TOK = 128
GROUP = 1024
KCHUNK = 1024
EPSILON = 1e-06
NEGATIVE = -1e30
LOG2E = 1.4426950408889634
SCALE = HDIM ** (-0.5)
F32 = jnp.float32
BF16 = jnp.bfloat16


def nt(left, right):
    return lax.dot_general(left, right, (((1,), (1,)), ((), ())), preferred_element_type=F32)


def nn(left, right):
    return lax.dot_general(left, right, (((1,), (0,)), ((), ())), preferred_element_type=F32)


def norm_of(ref, gain_ref, row):
    wide = ref[...].astype(F32)
    inverse = lax.rsqrt(jnp.mean(wide * wide, axis=1, keepdims=True) + EPSILON)
    return (wide * inverse * gain_ref[row : row + 1, :]).astype(BF16)


def put(out_ref, slot, rows, first=0, flip=None):
    for head in range(out_ref.shape[0]):
        piece = rows[:, (first + head) * HDIM : (first + head + 1) * HDIM]
        if flip is None:
            out_ref[head, slot] = piece
        else:
            out_ref[lax.bitwise_xor(jnp.int32(head), flip), slot] = piece


def pack_first_kernel(k_ref, v_ref, gain_ref, kv_ref):
    put(kv_ref, 0, norm_of(k_ref, gain_ref, 1))
    put(kv_ref, 1, v_ref[...])


def pack_rest_kernel(place_ref, k_ref, v_ref, q_ref, g_ref, gain_ref, qg_ref, b_ref):
    flip = place_ref[0]
    queries = norm_of(q_ref, gain_ref, 0)
    keys = norm_of(k_ref, gain_ref, 1)
    cotangents = g_ref[...]
    first = qg_ref.shape[0]
    put(qg_ref, 0, queries)
    put(qg_ref, 1, cotangents)
    put(b_ref, 0, keys, first, flip)
    put(b_ref, 1, v_ref[...], 0, flip)
    put(b_ref, 2, queries, first, flip)
    put(b_ref, 3, cotangents, first, flip)


def slabs_of(heads, slots, step):
    return pl.BlockSpec((heads, slots, step, HDIM), lambda i: (0, 0, i, 0))


def pack_first(key_pre, values, gain_full, heads_a):
    tokens, channels = key_pre.shape
    step = 32
    return pl.pallas_call(
        pack_first_kernel,
        grid=(tokens // step,),
        in_specs=[
            pl.BlockSpec((step, channels), lambda i: (i, 0)),
            pl.BlockSpec((step, heads_a * HDIM), lambda i: (i, 0)),
            pl.BlockSpec((2, channels), lambda i: (0, 0)),
        ],
        out_specs=slabs_of(heads_a, 2, step),
        out_shape=jax.ShapeDtypeStruct((heads_a, 2, tokens, HDIM), BF16),
        name="pack_first",
        cost_estimate=pl.CostEstimate(
            flops=5 * tokens * channels, bytes_accessed=6 * tokens * channels, transcendentals=tokens
        ),
    )(key_pre, values, gain_full)


def pack_rest(place, key_pre, values, query_pre, cotangent, gain_full, heads_a):
    tokens, channels = query_pre.shape
    heads_b = channels // HDIM - heads_a
    step = 32
    rows = pl.BlockSpec((step, channels), lambda i: (i, 0))
    rest = pl.BlockSpec((step, heads_b * HDIM), lambda i: (i, heads_a // heads_b))
    return pl.pallas_call(
        pack_rest_kernel,
        grid=(tokens // step,),
        in_specs=[pl.BlockSpec(memory_space=pltpu.SMEM), rows, rest, rows, rows]
        + [pl.BlockSpec((2, channels), lambda i: (0, 0))],
        out_specs=[slabs_of(heads_a, 2, step), slabs_of(heads_b, 4, step)],
        out_shape=[
            jax.ShapeDtypeStruct((heads_a, 2, tokens, HDIM), BF16),
            jax.ShapeDtypeStruct((heads_b, 4, tokens, HDIM), BF16),
        ],
        name="pack_rest",
        cost_estimate=pl.CostEstimate(
            flops=10 * tokens * channels, bytes_accessed=12 * tokens * channels, transcendentals=2 * tokens
        ),
    )(place, key_pre, values, query_pre, cotangent, gain_full)


def gather_kernel(place_ref, *refs):
    ins, (kv_ref, qg_ref) = refs[:-2], refs[-2:]
    for step, ref in enumerate(ins):
        at = lax.bitwise_xor(jnp.int32(step), place_ref[0])
        kv_ref[at] = ref[0, 0:2]
        qg_ref[at] = ref[0, 2:4]


def gather(place, parts):
    count = len(parts)
    shape = (count, 2, TOK, HDIM)
    whole = pl.BlockSpec(shape, lambda i: (0, 0, 0, 0))
    return pl.pallas_call(
        gather_kernel,
        grid=(1,),
        in_specs=[pl.BlockSpec(memory_space=pltpu.SMEM)]
        + [pl.BlockSpec((1, 4, TOK, HDIM), lambda i: (0, 0, 0, 0))] * count,
        out_specs=[whole, whole],
        out_shape=[jax.ShapeDtypeStruct(shape, BF16)] * 2,
        name="gather",
        cost_estimate=pl.CostEstimate(flops=0, bytes_accessed=count * TOK * HDIM * 16, transcendentals=0),
    )(place, *parts)


def unit_kernel(
    line, info_ref, q_ref, g_ref, ko_ref, vo_ref, kp_ref, vp_ref,
    dq_ref, dko_ref, dvo_ref, back_ref, gain_ref,
    p_ref, dp_ref,
):
    chunks = 2 * GROUP // KCHUNK
    own_chunks = GROUP // KCHUNK

    def part_of(own_ref, prev_ref, chunk):
        ref = own_ref if chunk < own_chunks else prev_ref
        first = chunk % own_chunks * KCHUNK // TOK
        return ref[first : first + KCHUNK // TOK].reshape(KCHUNK, HDIM)

    keys_at = functools.partial(part_of, ko_ref, kp_ref)
    values_at = functools.partial(part_of, vo_ref, vp_ref)
    bound = info_ref[line, 0]
    is_open = info_ref[line, 1] > 0
    early_weight = info_ref[line, 2].astype(F32)
    late_weight = info_ref[line, 3].astype(F32)
    q = q_ref[...].reshape(GROUP, HDIM)
    g = g_ref[...].reshape(GROUP, HDIM)
    early = lax.broadcasted_iota(jnp.int32, (1, GROUP), 1) < bound
    reach = jnp.where(early, bound, GROUP)
    weight = jnp.where(early, early_weight, late_weight)
    factor = SCALE * LOG2E

    pieces = []
    for chunk in range(chunks):
        span = slice(chunk * KCHUNK, (chunk + 1) * KCHUNK)
        scores = nt(keys_at(chunk), q)
        if chunk < own_chunks and (chunk + 1) * KCHUNK > GROUP // 4:
            row = chunk * KCHUNK + lax.broadcasted_iota(jnp.int32, (KCHUNK, GROUP), 0)
            scores = jnp.where(row < reach, scores, NEGATIVE)
        top = jnp.max(scores, axis=0, keepdims=True) * factor
        probs = jnp.exp2(scores * factor - top)
        grads = nt(values_at(chunk), g)
        p_ref[span] = probs
        dp_ref[span] = grads
        if chunk >= own_chunks:
            top = jnp.where(is_open, top, NEGATIVE)
        pieces.append((top, jnp.sum(probs, axis=0, keepdims=True), jnp.sum(probs * grads, axis=0, keepdims=True)))
    row_max = functools.reduce(jnp.maximum, [piece[0] for piece in pieces])
    lifts = [jnp.exp2(piece[0] - row_max) for piece in pieces]
    total = sum(lift * piece[1] for lift, piece in zip(lifts, pieces))
    inner = sum(lift * piece[2] for lift, piece in zip(lifts, pieces))
    over = 1.0 / total
    delta = inner * over
    dq_t = jnp.zeros((HDIM, GROUP), F32)
    for chunk in range(chunks):
        span = slice(chunk * KCHUNK, (chunk + 1) * KCHUNK)
        weights = p_ref[span] * (weight * over * lifts[chunk])
        sgrad = (weights * (dp_ref[span] - delta)).astype(BF16)
        dk = nn(sgrad, q) * SCALE
        dv = nn(weights.astype(BF16), g)
        if chunk < own_chunks:
            dko_ref[span] = dk
            dvo_ref[span] = dv
        else:
            back_ref[chunk * KCHUNK - GROUP : (chunk + 1) * KCHUNK - GROUP] = dk.astype(BF16)
            back_ref[chunk * KCHUNK : (chunk + 1) * KCHUNK] = dv.astype(BF16)
        dq_t = dq_t + nn(keys_at(chunk).T, sgrad)
    dq = (dq_t * SCALE).T
    gain_ref[...] = jnp.broadcast_to(jnp.sum(dq * q.astype(F32), axis=0, keepdims=True), (8, HDIM))
    dq_ref[...] = dq.astype(BF16)


def unit(line, info, sources):
    slabs = GROUP // TOK

    def whole(source):
        _, at, slot = source
        return pl.BlockSpec((slabs, None, TOK, HDIM), lambda i: (at, slot, 0, 0))

    full = pl.BlockSpec((GROUP, HDIM), lambda i: (0, 0))
    return pl.pallas_call(
        functools.partial(unit_kernel, line),
        grid=(1,),
        in_specs=[pl.BlockSpec(memory_space=pltpu.SMEM)]
        + [whole(source) for source in sources],
        out_specs=[
            full, full, full,
            pl.BlockSpec((2 * GROUP, HDIM), lambda i: (0, 0)),
            pl.BlockSpec((8, HDIM), lambda i: (0, 0)),
        ],
        out_shape=[
            jax.ShapeDtypeStruct((GROUP, HDIM), BF16),
            jax.ShapeDtypeStruct((GROUP, HDIM), F32),
            jax.ShapeDtypeStruct((GROUP, HDIM), F32),
            jax.ShapeDtypeStruct((2 * GROUP, HDIM), BF16),
            jax.ShapeDtypeStruct((8, HDIM), F32),
        ],
        scratch_shapes=[
            pltpu.VMEM((2 * GROUP, GROUP), F32),
            pltpu.VMEM((2 * GROUP, GROUP), F32),
        ],
        cost_estimate=pl.CostEstimate(
            flops=20 * GROUP * GROUP * HDIM, bytes_accessed=3 << 20, transcendentals=2 * GROUP * GROUP
        ),
    )(info, *[source[0] for source in sources])


def combine_kernel(groups, *refs):
    ins, out_ref = refs[: 4 * groups], refs[-1]
    slabs = out_ref.shape[0] // groups
    for group in range(groups):
        dq, dk, dv, back = ins[4 * group : 4 * group + 4]
        at = slice(group * slabs, (group + 1) * slabs)
        out_ref[at, :TOK] = dq[...].reshape(slabs, TOK, HDIM)
        out_ref[at, TOK : 2 * TOK] = (dk[...] + back[:GROUP].astype(F32)).astype(BF16).reshape(slabs, TOK, HDIM)
        out_ref[at, 2 * TOK : 3 * TOK] = (dv[...] + back[GROUP:].astype(F32)).astype(BF16).reshape(slabs, TOK, HDIM)


def combine(parts):
    groups = len(parts)
    slabs = groups * GROUP // TOK
    flat = [array for part in parts for array in part]
    full = pl.BlockSpec((GROUP, HDIM), lambda i: (0, 0))
    back = pl.BlockSpec((2 * GROUP, HDIM), lambda i: (0, 0))
    specs = [full, full, full, back] * groups
    depth = 3 * TOK
    return pl.pallas_call(
        functools.partial(combine_kernel, groups),
        grid=(1,),
        in_specs=specs,
        out_specs=pl.BlockSpec((slabs, depth, HDIM), lambda i: (0, 0, 0)),
        out_shape=jax.ShapeDtypeStruct((slabs, depth, HDIM), BF16),
        cost_estimate=pl.CostEstimate(
            flops=10 * groups * GROUP * HDIM, bytes_accessed=groups * GROUP * HDIM * 20, transcendentals=0
        ),
    )(*flat)


def finish_kernel(heads_a, heads_b, x_ref, y_ref, gain_ref, *refs):
    blocks, (qg_ref, kg_ref, vg_ref) = refs[:6], refs[6:]
    channels = x_ref.shape[1]

    def piece(head, slot):
        return blocks[slot][head] if head < heads_a else blocks[3 + slot][head - heads_a]

    for slot, ref, out in ((0, x_ref, qg_ref), (1, y_ref, kg_ref)):
        wide = ref[...].astype(F32)
        inverse = lax.rsqrt(jnp.mean(wide * wide, axis=1, keepdims=True) + EPSILON)
        normal = wide * inverse
        up = jnp.concatenate([piece(h, slot).astype(F32) for h in range(heads_a + heads_b)], axis=1)
        scaled = up * gain_ref[slot : slot + 1, :]
        inner = jnp.sum(scaled * normal, axis=1, keepdims=True) * (1.0 / channels)
        out[...] = (inverse * (scaled - normal * inner)).astype(BF16)
    for head in range(heads_a + heads_b):
        vg_ref[:, head * HDIM : (head + 1) * HDIM] = piece(head, 2)


def finish(query_pre, key_pre, gain_full, home_a, home_b):
    tokens, channels = query_pre.shape
    heads_a, heads_b = home_a.shape[0], home_b.shape[0]
    step = 32
    rows = pl.BlockSpec((step, channels), lambda i: (i, 0))

    def block(heads, slot):
        return pl.BlockSpec((heads, step, HDIM), lambda i: (0, slot * (tokens // step) + i, 0))

    return pl.pallas_call(
        functools.partial(finish_kernel, heads_a, heads_b),
        grid=(tokens // step,),
        in_specs=[rows, rows, pl.BlockSpec((2, channels), lambda i: (0, 0))]
        + [block(heads_a, slot) for slot in range(3)]
        + [block(heads_b, slot) for slot in range(3)],
        out_specs=[rows] * 3,
        out_shape=[jax.ShapeDtypeStruct((tokens, channels), BF16)] * 3,
        name="finish",
        cost_estimate=pl.CostEstimate(
            flops=30 * tokens * channels, bytes_accessed=16 * tokens * channels, transcendentals=tokens
        ),
    )(query_pre, key_pre, gain_full, home_a, home_a, home_a, home_b, home_b, home_b)


def shifted(value, steps, count):
    first, last = (max(0, -steps), min(count, count - steps))
    return lax.ppermute(value, "span", [(source, source + steps) for source in range(first, last)])


def swapped(value, axis, bit, count):
    return lax.ppermute(value, axis, [(i, i ^ bit) for i in range(count)])


def lines_of(bound, other, span, table):
    odd = span % 2
    even = span - odd
    row = lax.iota(jnp.int32, 3)
    groups = jnp.where(row == 0, span, even + row - 1)
    bounds = jnp.where((row == 0) | (groups == span), bound, other)
    spans = 2 * groups[:, None] + lax.iota(jnp.int32, 8)[None, :] - 2
    match = spans[:, :, None] == lax.iota(jnp.int32, table.shape[0])[None, None, :]
    weights = jnp.sum(jnp.where(match, table[None, None, :], 0), axis=2)
    column = lax.iota(jnp.int32, 8)[None, :]
    opens = (groups > 0).astype(jnp.int32)
    return jnp.where(column == 0, bounds[:, None], jnp.where(column == 1, opens[:, None], weights))


def on_device(query_pre, key_pre, values, cotangent, gains, frame_span, denoise_steps):
    n_span, n_sp = lax.axis_size("span"), lax.axis_size("sp")
    heads_a = 2 * n_sp
    slabs = GROUP // TOK
    plane = [[first + i for i in range(heads_a)] for first in range(0, n_span * n_sp, heads_a)]

    def to_plane(value):
        return lax.all_to_all(
            value, ("span", "sp"), split_axis=0, concat_axis=0, tiled=True, axis_index_groups=plane
        )

    def to_sp(value):
        return lax.all_to_all(value, "sp", split_axis=0, concat_axis=0, tiled=True)

    span = lax.axis_index("span")
    other_gains = swapped(gains, "fsdp", 1, 2)
    first_half = lax.axis_index("fsdp") == 0
    gain_full = jnp.concatenate(
        [jnp.where(first_half, gains, other_gains), jnp.where(first_half, other_gains, gains)], axis=1
    )
    send_kv = pack_first(key_pre[0], values[0], gain_full, heads_a)
    kv = to_plane(send_kv)
    place = lax.axis_index("sp").reshape(1)
    send_qg, send_b = pack_rest(place, key_pre[0], values[0], query_pre[0], cotangent[0], gain_full, heads_a)
    qg = to_plane(send_qg)
    parts = [send_b[0:1]]
    for bits in range(1, n_sp):
        parts.append(swapped(send_b[bits : bits + 1], "sp", bits, n_sp))
    kv_own, qg_own = gather(place, parts)

    ids = frame_span[0]
    bound = jnp.sum((ids == ids[0]).astype(jnp.int32))
    other = swapped(jnp.full((8, HDIM), bound, F32), "span", 1, n_span)
    info = lines_of(bound, other[0, 0].astype(jnp.int32), span, denoise_steps[0])

    prev_a = shifted(kv[slabs:], 2, n_span)
    dq_e, dk_e, dv_e, term_e, gain_e = unit(
        1, info, [(qg, 0, 0), (qg, 0, 1), (kv, 0, 0), (kv, 0, 1), (prev_a, 0, 0), (prev_a, 0, 1)]
    )
    dq_o, dk_o, dv_o, term_o, gain_o = unit(
        2, info, [(qg, 1, 0), (qg, 1, 1), (kv, 1, 0), (kv, 1, 1), (kv, 0, 0), (kv, 0, 1)]
    )
    back_a = shifted(term_e, -2, n_span)
    out_a = combine([(dq_e, dk_e, dv_e, term_o), (dq_o, dk_o, dv_o, back_a)])
    home_a = to_plane(out_a)

    prev_b = shifted(kv_own, 1, n_span)
    dq_b, dk_b, dv_b, term_b, gain_b = unit(
        0, info, [(qg_own, 0, 0), (qg_own, 0, 1), (kv_own, 0, 0), (kv_own, 0, 1), (prev_b, 0, 0), (prev_b, 0, 1)]
    )
    back_b = shifted(term_b, -1, n_span)

    out_b = combine([(dq_b, dk_b, dv_b, back_b)])
    home_b = to_sp(out_b)

    share = jnp.concatenate([gain_e[0:1] + gain_o[0:1], gain_b[0:1], jnp.zeros((6, HDIM), F32)], axis=0)
    share = share + swapped(share, "fsdp", 1, 2)
    terms = [share]
    for reach in range(4, n_span, 4):
        terms.append(lax.ppermute(share, "span", [(i, (i + reach) % n_span) for i in range(n_span)]))
    share = sum(terms[1:], terms[0])
    near = [share]
    for bits in (1, 2, 3):
        near.append(swapped(share, "span", bits, n_span))
    here, there = near[0] + near[2], near[1] + near[3]
    even = span % 2 == 0
    share = jnp.concatenate(
        [
            jnp.where(even, here[0:1], there[0:1]),
            jnp.where(even, there[0:1], here[0:1]),
            here[1:2] + there[1:2],
            jnp.zeros((5, HDIM), F32),
        ],
        axis=0,
    )
    lines = to_sp(jnp.broadcast_to(share[None], (n_sp, 8, HDIM)))
    table = lines[:, :GAIN_ROWS].transpose(1, 0, 2).reshape(GAIN_ROWS * n_sp, HDIM)
    half = GAIN_ROWS * n_sp >> 1
    mine = jnp.where(first_half, table[:half], table[half:]).reshape(1, half * HDIM)
    gain_grad = mine / gains

    query_back, key_back, value_back = finish(query_pre[0], key_pre[0], gain_full, home_a, home_b)
    return (query_back[None], key_back[None], value_back[None], gain_grad)


def solution(mesh):
    rows = P("fsdp", ("span", "sp"), None)
    return jax.shard_map(
        on_device,
        mesh=mesh,
        in_specs=(rows, rows, rows, rows, P(None, "fsdp"), P("fsdp", "span"), P("fsdp", None)),
        out_specs=(rows, rows, rows, P(None, "fsdp")),
        check_vma=False,
    )
```
